512 devices in a mesh: ex: 32 (over y, x, core), mp: 16 (over z).
Axes of the slice: x: 4, y: 4, z: 16, core: 2. Of those that a mesh axis runs over, the one named last changes fastest.
Arguments:
- acts: bfloat16 [16, 4096, 4096], P('mp', 'ex'), may hold values from -6 to 6
- grads: bfloat16 [16, 4096, 1024], P('mp', 'ex'), may hold values from -12 to 12
- down_factor: bfloat16 [16, 16, 4096], P('mp'), may hold values from -0.09375 to 0.09375
- up_factor_transposed: bfloat16 [16, 16, 1024], P('mp'), may hold values from -0.1875 to 0.1875
- input_projection: bfloat16 [16, 64, 4096], P('mp'), may hold values from -0.09375 to 0.09375
- gradient_projection: bfloat16 [16, 64, 1024], P('mp'), may hold values from -0.1875 to 0.1875
- order: int32 [16, 32, 16], P('mp', 'ex'), may hold values from 0 to 15, each once within a row
- damping: float32 [1], replicated, may hold values from 0.5 to 2
Outputs:
- features: float32 [512, 1024], P(('ex', 'mp'))
- factor_r: float32 [16, 64, 64], P('mp')
The draws below stay inside these ranges and needn't reach their ends.
Inputs may be any that keep to these rules, and one draw needn't show every extreme that they name: order[b, m] lists each of the 16 examples of shard m once: stored example e of block b is example order[b, m, e] of that shard.
All inputs are finite; a program needn't handle non-finite values.
Results may differ from the reference program's by a relative error of at most 0.0003.
Values sent between devices are 32-bit elements; how exact they have to be, the bound alone decides.
A program may use at most 64 MiB of HBM per device.

```python
import math
import jax
import jax.numpy as jnp
from jax import lax

MODEL_WIDTH = 4096
KEY_WIDTH = 1024
ADAPTER_RANK = 16
KP = 64
E_DEV = 16
EXAMPLE_LENGTH = 8
LAYER_BLOCKS = 16
SHARDS = 32
TOKENS = 4096
EXAMPLES = 512


def draw_grads(key, part):
    key_base, key_scale = jax.random.split(key, 2)
    stored = TOKENS // EXAMPLE_LENGTH
    logs = jax.random.uniform(key_scale, (LAYER_BLOCKS, stored, 1), jnp.float32, math.log(0.3), math.log(3.0))
    scaling = jnp.repeat(jnp.exp(logs), EXAMPLE_LENGTH, axis=1)
    base = jax.random.normal(key_base, (LAYER_BLOCKS, TOKENS, KEY_WIDTH), jnp.float32)
    return jnp.clip(base * scaling, -12.0, 12.0).astype(jnp.bfloat16)


def levels(stream_key, shape, shards, low, top_value):
    loudness, own = 1.0, jax.random.fold_in(stream_key, 6)
    for axis_at, parts in shards:
        heights = jnp.exp(jax.random.uniform(jax.random.fold_in(own, axis_at), (parts,), jnp.float32, low / len(shards), top_value / len(shards)))
        loudness = loudness * jnp.repeat(heights, shape[axis_at] // parts).reshape([-1 if axis == axis_at else 1 for axis in range(len(shape))])
    return loudness


def gaussian(key, extent, width, limit, pieces=(), held_as=jnp.bfloat16):
    gain = levels(key, extent, pieces, -0.22, 0.18) if pieces else 1.0
    array = jax.random.normal(key, extent, jnp.float32) * width * gain
    return jnp.minimum(jnp.maximum(array, -limit), limit).astype(held_as)


def setup_inputs(seed: int = 0) -> dict:
    streams_of = jax.random.split(jax.random.key(seed), 9)
    acts = gaussian(streams_of[0], (LAYER_BLOCKS, TOKENS, MODEL_WIDTH), 1.0, 6.0, ((0, 16), (1, 32)))
    grads = draw_grads(jax.random.fold_in(streams_of[8], 71), 0)
    down_factor = gaussian(streams_of[2], (LAYER_BLOCKS, ADAPTER_RANK, MODEL_WIDTH), MODEL_WIDTH ** -0.5, 0.09375, ((0, 16),))
    up_factor_transposed = gaussian(streams_of[3], (LAYER_BLOCKS, ADAPTER_RANK, KEY_WIDTH), KEY_WIDTH ** -0.5, 0.1875, ((0, 16),))
    input_projection = gaussian(streams_of[4], (LAYER_BLOCKS, KP, MODEL_WIDTH), MODEL_WIDTH ** -0.5, 0.09375, ((0, 16),))
    gradient_projection = gaussian(streams_of[5], (LAYER_BLOCKS, KP, KEY_WIDTH), KEY_WIDTH ** -0.5, 0.1875, ((0, 16),))
    order = jax.vmap(lambda own: jax.random.permutation(own, E_DEV))(jax.random.split(streams_of[6], LAYER_BLOCKS * SHARDS)).reshape((LAYER_BLOCKS, SHARDS, E_DEV)).astype(jnp.int32)
    damping = jnp.clip(jnp.exp(jax.random.uniform(streams_of[7], (1,), jnp.float32, math.log(0.5), math.log(2.0))), 0.5, 2.0)
    return dict(acts=acts, grads=grads, down_factor=down_factor, up_factor_transposed=up_factor_transposed, input_projection=input_projection, gradient_projection=gradient_projection, order=order, damping=damping)


def block_partial(input_rows, output_gradients, weight_a, weight_b, sketch_a, sketch_g):
    reduced_gradient = jnp.dot(output_gradients.astype(jnp.float32), weight_b.T.astype(jnp.float32), preferred_element_type=jnp.float32)
    reduced_input = jnp.dot(input_rows.astype(jnp.float32), weight_a.T.astype(jnp.float32), preferred_element_type=jnp.float32)
    sketch_in = jnp.dot(input_rows.astype(jnp.float32), sketch_a.T.astype(jnp.float32), preferred_element_type=jnp.float32)
    sketch_out = jnp.dot(output_gradients.astype(jnp.float32), sketch_g.T.astype(jnp.float32), preferred_element_type=jnp.float32)
    reduced_gradient = reduced_gradient.reshape(EXAMPLES, EXAMPLE_LENGTH, ADAPTER_RANK)
    reduced_input = reduced_input.reshape(EXAMPLES, EXAMPLE_LENGTH, ADAPTER_RANK)
    sketch_in = sketch_in.reshape(EXAMPLES, EXAMPLE_LENGTH, KP)
    sketch_out = sketch_out.reshape(EXAMPLES, EXAMPLE_LENGTH, KP)
    first = jnp.einsum('etc,etk->eck', reduced_gradient, sketch_in, precision=lax.Precision.HIGHEST)
    second = jnp.einsum('etc,etk->eck', reduced_input, sketch_out, precision=lax.Precision.HIGHEST)
    return (first + second).reshape(EXAMPLES, ADAPTER_RANK * KP)

def reference(acts, grads, down_factor, up_factor_transposed, input_projection, gradient_projection, order, damping):
    feature_width = ADAPTER_RANK * KP
    scaling = 1.0 / math.sqrt(2.0 * EXAMPLE_LENGTH * LAYER_BLOCKS)
    offsets = (jnp.arange(SHARDS, dtype=jnp.int32) * E_DEV)[:, None]

    def single_block(carry, items):
        input_rows, output_gradients, weight_a, weight_b, sketch_a, sketch_g, ordering = items
        partial_value = block_partial(input_rows, output_gradients, weight_a, weight_b, sketch_a, sketch_g) * scaling
        target = (offsets + ordering.astype(jnp.int32)).reshape(-1).astype(jnp.int32)
        placed = jnp.zeros((EXAMPLES, feature_width), jnp.float32).at[target].set(partial_value)
        return (carry + placed, None)
    start_offset = jnp.zeros((EXAMPLES, feature_width), jnp.float32)
    features, unused_value = lax.scan(single_block, start_offset, (acts, grads, down_factor, up_factor_transposed, input_projection, gradient_projection, order))
    grouped = features.reshape(EXAMPLES, ADAPTER_RANK, KP)
    gram_blocks = jnp.einsum('eck,ecl->ckl', grouped, grouped, precision=lax.Precision.HIGHEST)
    system = gram_blocks / EXAMPLES + damping[0] * jnp.eye(KP, dtype=jnp.float32)[None, :, :]
    factor_r = jnp.swapaxes(jnp.linalg.cholesky(system), 1, 2)
    return (features, factor_r)
```

```python
import functools
import math

import jax
import jax.numpy as jnp
from jax import lax
from jax.experimental import pallas as pl
from jax.experimental.pallas import tpu as pltpu
from jax.sharding import PartitionSpec as P

EXAMPLE_LENGTH = 8
CHUNKS = 4
MESH = pl.DeviceIdType.MESH


def nt(a, b):
    return lax.dot_general(a, b, (((1,), (1,)), ((), ())), preferred_element_type=jnp.float32)


def halves(x):
    high = x.astype(jnp.bfloat16)
    return high, (x - high.astype(jnp.float32)).astype(jnp.bfloat16)


def outward(step, n):
    turn = lax.rem(step + 1, 2)
    return n // 2 + ((step + 1) // 2) * (1 - 2 * turn)


def wait_bytes(buf, count, sem):
    part = buf.at[pl.ds(0, count)]
    pltpu.make_async_copy(part, part, sem).wait()


def factor(blocks, r_ref, size):
    lane = lax.broadcasted_iota(jnp.int32, (1, size), 1)
    blocks = list(blocks)
    for k in range(size):
        at, sub = k // 8, k % 8
        row = blocks[at][sub : sub + 1, :]
        pivot = row[:, k : k + 1]
        r_ref[0, k : k + 1, :] = jnp.where(lane >= k, row * lax.rsqrt(pivot), 0.0)
        if k + 1 < size:
            scaled = row * (1.0 / pivot)
            for b in range((k + 1) // 8, size // 8):
                blocks[b] = blocks[b] - blocks[b][:, k : k + 1] * scaled


def kernel(
    n_ex,
    n_mp,
    scaling,
    acts,
    grads,
    down,
    up,
    in_proj,
    g_proj,
    order,
    damping,
    out_f,
    out_r,
    a_v,
    g_v,
    wa_v,
    wg_v,
    zsend,
    zrecv,
    fbuf,
    xbuf,
    rowsend,
    rowrecv,
    load_sem,
    send_sem,
    recv_sem,
):
    ex = lax.axis_index("ex")
    mp = lax.axis_index("mp")
    rank = down.shape[1]
    sketch = in_proj.shape[1]
    width = a_v.shape[1] // CHUNKS

    g_copies = [
        pltpu.make_async_copy(up.at[0], wg_v.at[pl.ds(0, rank)], load_sem.at[0]),
        pltpu.make_async_copy(g_proj.at[0], wg_v.at[pl.ds(rank, sketch)], load_sem.at[1]),
        pltpu.make_async_copy(grads.at[0], g_v, load_sem.at[2]),
    ]
    a_copies = []
    for i in range(CHUNKS):
        cols = pl.ds(i * width, width)
        a_copies.append(
            [
                pltpu.make_async_copy(
                    down.at[0, :, cols], wa_v.at[pl.ds(0, rank), cols], load_sem.at[3 + 3 * i]
                ),
                pltpu.make_async_copy(
                    in_proj.at[0, :, cols], wa_v.at[pl.ds(rank, sketch), cols], load_sem.at[4 + 3 * i]
                ),
                pltpu.make_async_copy(acts.at[0, :, cols], a_v.at[:, cols], load_sem.at[5 + 3 * i]),
            ]
        )
    for copy in g_copies:
        copy.start()
    for chunk in a_copies:
        for copy in chunk:
            copy.start()

    barrier = pltpu.get_barrier_semaphore()

    def greet(axis, n, me):
        def body(s, _):
            dst = lax.rem(me + outward(s, n), n)
            pl.semaphore_signal(barrier, inc=1, device_id={axis: dst}, device_id_type=MESH)
            return 0

        lax.fori_loop(0, n - 1, body, 0)

    greet("mp", n_mp, mp)
    greet("ex", n_ex, ex)

    tokens = a_v.shape[0]
    spread = (
        lax.broadcasted_iota(jnp.int32, (rank, tokens), 1) // EXAMPLE_LENGTH
        == lax.broadcasted_iota(jnp.int32, (rank, tokens), 0)
    ).astype(jnp.float32)
    stored = jnp.broadcast_to(order[0].astype(jnp.float32), (16, 16)).astype(jnp.bfloat16)
    target = lax.dot_general(
        stored,
        spread.astype(jnp.bfloat16),
        (((1,), (0,)), ((), ())),
        preferred_element_type=jnp.float32,
    )
    rows = lax.broadcasted_iota(jnp.int32, (16, tokens), 0).astype(jnp.float32)
    place = jnp.where(target == rows, scaling, 0.0)

    for copy in g_copies:
        copy.wait()
    from_g = nt(wg_v[...], g_v[...])
    from_a = jnp.zeros((rank + sketch, tokens), jnp.float32)
    for i in range(CHUNKS):
        for copy in a_copies[i]:
            copy.wait()
        cols = slice(i * width, (i + 1) * width)
        from_a = from_a + nt(wa_v[:, cols], a_v[:, cols])

    low = [from_g[:rank], from_a[:rank]]
    left = jnp.concatenate(
        [
            jnp.concatenate(
                [
                    (x[:, None, :] * place[None, h * 8 : h * 8 + 8]).reshape(rank * 8, tokens)
                    for x in low
                ],
                axis=1,
            )
            for h in range(2)
        ],
        axis=0,
    )
    right = jnp.concatenate([from_a[rank:], from_g[rank:]], axis=1)
    left_h, left_l = halves(left)
    right_h, right_l = halves(right)
    part = nt(left_h, right_h) + (nt(left_h, right_l) + nt(left_l, right_h))
    tiles = jnp.concatenate([part[: rank * 8], part[rank * 8 :]], axis=1)
    zsend[...] = tiles.reshape(rank, 8, 2 * sketch)

    pl.semaphore_wait(barrier, n_mp + n_ex - 2)

    def send_z(s, _):
        dst = lax.rem(mp + outward(s, n_mp), n_mp)
        pltpu.make_async_remote_copy(
            src_ref=zsend.at[dst],
            dst_ref=zrecv.at[mp],
            send_sem=send_sem.at[0],
            recv_sem=recv_sem.at[0],
            device_id={"mp": dst},
            device_id_type=MESH,
        ).start()
        return 0

    lax.fori_loop(0, n_mp - 1, send_z, 0)
    zrecv[mp] = zsend[mp]
    wait_bytes(zrecv, n_mp - 1, recv_sem.at[0])
    mine = jnp.sum(zrecv[...], axis=0)
    fbuf[...] = mine
    xbuf[ex] = mine

    def send_x(s, _):
        dst = lax.rem(ex + outward(s, n_ex), n_ex)
        pltpu.make_async_remote_copy(
            src_ref=fbuf,
            dst_ref=xbuf.at[ex],
            send_sem=send_sem.at[1],
            recv_sem=recv_sem.at[1],
            device_id={"ex": dst},
            device_id_type=MESH,
        ).start()
        return 0

    lax.fori_loop(0, n_ex - 1, send_x, 0)

    lane = lax.broadcasted_iota(jnp.int32, (8, 2 * sketch), 1)
    turned = jnp.concatenate([mine[:, sketch:], mine[:, :sketch]], axis=1)
    lower = jnp.where(lane < sketch, mine, turned)
    upper = jnp.where(lane < sketch, turned, mine)
    for r in range(8):
        rowsend[r] = lower[r : r + 1]
        rowsend[r + 8] = upper[r : r + 1]

    def send_rows(s, _):
        dst = lax.rem(mp + outward(s, n_mp), n_mp)
        pltpu.make_async_remote_copy(
            src_ref=rowsend.at[dst],
            dst_ref=rowrecv.at[mp],
            send_sem=send_sem.at[2],
            recv_sem=recv_sem.at[2],
            device_id={"mp": dst},
            device_id_type=MESH,
        ).start()
        return 0

    lax.fori_loop(0, n_mp - 1, send_rows, 0)
    rowrecv[mp] = rowsend[mp]

    wait_bytes(xbuf, n_ex - 1, recv_sem.at[1])
    every = xbuf[...].reshape(n_ex * 8, 2 * sketch)
    square = lax.dot_general(
        every,
        every,
        (((0,), (0,)), ((), ())),
        preferred_element_type=jnp.float32,
        precision=lax.Precision.HIGHEST,
    )
    gram = square[:sketch, :sketch] + square[sketch:, sketch:]
    diag = lax.broadcasted_iota(jnp.int32, (sketch, sketch), 0) == lax.broadcasted_iota(
        jnp.int32, (sketch, sketch), 1
    )
    system = gram * (1.0 / (n_ex * 16)) + jnp.where(diag, damping[0], 0.0)
    factor([system[b * 8 : b * 8 + 8] for b in range(sketch // 8)], out_r, sketch)

    wait_bytes(rowrecv, n_mp - 1, recv_sem.at[2])
    low_lane = lax.broadcasted_iota(jnp.int32, (1, 2 * sketch), 1) < sketch
    for p in range(rank // 2):
        out_f[:, p * 2 * sketch : (p + 1) * 2 * sketch] = jnp.where(
            low_lane, rowrecv[2 * p], rowrecv[2 * p + 1]
        )
    wait_bytes(zsend, n_mp - 1, send_sem.at[0])
    wait_bytes(xbuf, n_ex - 1, send_sem.at[1])
    wait_bytes(rowsend, n_mp - 1, send_sem.at[2])


def local(n_ex, n_mp, *args):
    acts, grads, down, up, in_proj, g_proj, order, damping = args
    rank, sketch = down.shape[1], in_proj.shape[1]
    scaling = 1.0 / math.sqrt(2.0 * EXAMPLE_LENGTH * n_mp)
    f32 = jnp.float32
    return pl.pallas_call(
        functools.partial(kernel, n_ex, n_mp, scaling),
        out_shape=(
            jax.ShapeDtypeStruct((1, rank * sketch), f32),
            jax.ShapeDtypeStruct((1, sketch, sketch), f32),
        ),
        in_specs=[pl.BlockSpec(memory_space=pl.ANY)] * 6
        + [
            pl.BlockSpec(memory_space=pltpu.VMEM),
            pl.BlockSpec(memory_space=pltpu.SMEM),
        ],
        out_specs=(
            pl.BlockSpec(memory_space=pltpu.VMEM),
            pl.BlockSpec(memory_space=pltpu.VMEM),
        ),
        scratch_shapes=[
            pltpu.VMEM(acts.shape[1:], acts.dtype),
            pltpu.VMEM(grads.shape[1:], grads.dtype),
            pltpu.VMEM((rank + sketch, acts.shape[2]), acts.dtype),
            pltpu.VMEM((rank + sketch, grads.shape[2]), grads.dtype),
            pltpu.VMEM((n_mp, 8, 2 * sketch), f32),
            pltpu.VMEM((n_mp, 8, 2 * sketch), f32),
            pltpu.VMEM((8, 2 * sketch), f32),
            pltpu.VMEM((n_ex, 8, 2 * sketch), f32),
            pltpu.VMEM((n_mp, 1, 2 * sketch), f32),
            pltpu.VMEM((n_mp, 1, 2 * sketch), f32),
            pltpu.SemaphoreType.DMA((3 + 3 * CHUNKS,)),
            pltpu.SemaphoreType.DMA((3,)),
            pltpu.SemaphoreType.DMA((3,)),
        ],
        compiler_params=pltpu.CompilerParams(collective_id=0, has_side_effects=True),
        name="trak",
    )(acts, grads, down, up, in_proj, g_proj, order, damping)


def solution(mesh):
    in_specs = (
        P("mp", "ex", None),
        P("mp", "ex", None),
        P("mp", None, None),
        P("mp", None, None),
        P("mp", None, None),
        P("mp", None, None),
        P("mp", "ex", None),
        P(),
    )
    out_specs = (P(("ex", "mp"), None), P("mp", None, None))
    body = functools.partial(local, mesh.shape["ex"], mesh.shape["mp"])
    return jax.shard_map(body, mesh=mesh, in_specs=in_specs, out_specs=out_specs, check_vma=False)
```

```python
import functools
import math

import jax
import jax.numpy as jnp
from jax import lax
from jax.experimental import pallas as pl
from jax.experimental.pallas import tpu as pltpu
from jax.sharding import PartitionSpec as P

EXAMPLE_LENGTH = 8
CHUNKS = 4
MESH = pl.DeviceIdType.MESH


def nt(a, b):
    return lax.dot_general(a, b, (((1,), (1,)), ((), ())), preferred_element_type=jnp.float32)


def halves(x):
    high = x.astype(jnp.bfloat16)
    return high, (x - high.astype(jnp.float32)).astype(jnp.bfloat16)


def outward(step, n):
    turn = lax.rem(step + 1, 2)
    return n // 2 + ((step + 1) // 2) * (1 - 2 * turn)


def wait_bytes(buf, count, sem):
    part = buf.at[pl.ds(0, count)]
    pltpu.make_async_copy(part, part, sem).wait()


def factor(blocks, r_ref, size):
    lane = lax.broadcasted_iota(jnp.int32, (8, size), 1)
    subl = lax.broadcasted_iota(jnp.int32, (8, size), 0)
    blocks = list(blocks)
    count = size // 8
    for q in range(count):
        k0 = q * 8
        top = blocks[q]
        cols = {
            b: [jnp.broadcast_to(blocks[b][:, k0 + j : k0 + j + 1], (8, size)) for j in range(8)]
            for b in range(q, count)
        }
        pivots = []
        rows = []
        scaled = []
        for j in range(8):
            pivot = jnp.broadcast_to(cols[q][j][j : j + 1, :], (8, size))
            inverse = 1.0 / pivot
            pivots.append(pivot)
            row = jnp.broadcast_to(top[j : j + 1, :], (8, size))
            step = row * inverse
            rows.append(row)
            scaled.append(step)
            top = top - cols[q][j] * step
            for i in range(j + 1, 8):
                ratio = jnp.broadcast_to(cols[q][i][j : j + 1, :], (8, size)) * inverse
                for b in range(q, count):
                    cols[b][i] = cols[b][i] - cols[b][j] * ratio
        whole, scale = rows[7], pivots[7]
        for j in range(7):
            whole = jnp.where(subl == j, rows[j], whole)
            scale = jnp.where(subl == j, pivots[j], scale)
        r_ref[0, k0 : k0 + 8, :] = jnp.where(lane >= subl + k0, whole * lax.rsqrt(scale), 0.0)
        for b in range(q + 1, count):
            for j in range(8):
                blocks[b] = blocks[b] - cols[b][j] * scaled[j]


def finish(gram, rowrecv, damping, out_f, out_r):
    size = gram.shape[0]
    diag = lax.broadcasted_iota(jnp.int32, (size, size), 0) == lax.broadcasted_iota(
        jnp.int32, (size, size), 1
    )
    full = gram[...] + jnp.where(diag, damping[0], 0.0)
    factor([full[b * 8 : b * 8 + 8] for b in range(size // 8)], out_r, size)
    low_lane = lax.broadcasted_iota(jnp.int32, (1, 2 * size), 1) < size
    for p in range(rowrecv.shape[0] // 2):
        out_f[:, p * 2 * size : (p + 1) * 2 * size] = jnp.where(
            low_lane, rowrecv[2 * p], rowrecv[2 * p + 1]
        )


def kernel(
    n_ex,
    n_mp,
    scaling,
    acts,
    grads,
    down,
    up,
    in_proj,
    g_proj,
    order,
    out_s,
    rowrecv,
    a_v,
    g_v,
    wa_v,
    wg_v,
    zsend,
    zrecv,
    fbuf,
    xbuf,
    rowsend,
    order_v,
    load_sem,
    send_sem,
    recv_sem,
):
    ex = lax.axis_index("ex")
    mp = lax.axis_index("mp")
    rank = down.shape[1]
    sketch = in_proj.shape[1]
    width = a_v.shape[1] // CHUNKS

    g_copies = [
        pltpu.make_async_copy(up.at[0], wg_v.at[pl.ds(0, rank)], load_sem.at[0]),
        pltpu.make_async_copy(g_proj.at[0], wg_v.at[pl.ds(rank, sketch)], load_sem.at[1]),
        pltpu.make_async_copy(grads.at[0], g_v, load_sem.at[2]),
    ]
    a_copies = []
    for i in range(CHUNKS):
        cols = pl.ds(i * width, width)
        a_copies.append(
            [
                pltpu.make_async_copy(
                    down.at[0, :, cols], wa_v.at[pl.ds(0, rank), cols], load_sem.at[3 + 3 * i]
                ),
                pltpu.make_async_copy(
                    in_proj.at[0, :, cols], wa_v.at[pl.ds(rank, sketch), cols], load_sem.at[4 + 3 * i]
                ),
                pltpu.make_async_copy(acts.at[0, :, cols], a_v.at[:, cols], load_sem.at[5 + 3 * i]),
            ]
        )
    order_copy = pltpu.make_async_copy(order, order_v, load_sem.at[3 + 3 * CHUNKS])

    barrier = pltpu.get_barrier_semaphore()

    def greet(axis, n, me):
        def body(s, _):
            dst = lax.rem(me + outward(s, n), n)
            pl.semaphore_signal(barrier, inc=1, device_id={axis: dst}, device_id_type=MESH)
            return 0

        lax.fori_loop(0, n - 1, body, 0)

    greet("mp", n_mp, mp)
    order_copy.start()
    for copy in g_copies:
        copy.start()
    for chunk in a_copies:
        for copy in chunk:
            copy.start()
    greet("ex", n_ex, ex)

    tokens = a_v.shape[0]
    spread = (
        lax.broadcasted_iota(jnp.int32, (rank, tokens), 1) // EXAMPLE_LENGTH
        == lax.broadcasted_iota(jnp.int32, (rank, tokens), 0)
    ).astype(jnp.float32)
    order_copy.wait()
    stored = jnp.broadcast_to(order_v[0].astype(jnp.float32), (16, 16)).astype(jnp.bfloat16)
    target = lax.dot_general(
        stored,
        spread.astype(jnp.bfloat16),
        (((1,), (0,)), ((), ())),
        preferred_element_type=jnp.float32,
    )
    rows = lax.broadcasted_iota(jnp.int32, (16, tokens), 0).astype(jnp.float32)
    place = jnp.where(target == rows, scaling, 0.0)

    for copy in g_copies:
        copy.wait()
    from_g = nt(wg_v[...], g_v[...])
    from_a = jnp.zeros((rank + sketch, tokens), jnp.float32)
    for i in range(CHUNKS):
        for copy in a_copies[i]:
            copy.wait()
        cols = slice(i * width, (i + 1) * width)
        from_a = from_a + nt(wa_v[:, cols], a_v[:, cols])

    low = [from_g[:rank], from_a[:rank]]
    left = jnp.concatenate(
        [
            jnp.concatenate(
                [
                    (x[:, None, :] * place[None, h * 8 : h * 8 + 8]).reshape(rank * 8, tokens)
                    for x in low
                ],
                axis=1,
            )
            for h in range(2)
        ],
        axis=0,
    )
    right = jnp.concatenate([from_a[rank:], from_g[rank:]], axis=1)
    left_h, left_l = halves(left)
    right_h, right_l = halves(right)
    part = nt(left_h, right_h) + (nt(left_h, right_l) + nt(left_l, right_h))
    tiles = jnp.concatenate([part[: rank * 8], part[rank * 8 :]], axis=1)
    zsend[...] = tiles.reshape(rank, 8, 2 * sketch)

    pl.semaphore_wait(barrier, n_mp + n_ex - 2)

    def send_z(s, _):
        dst = lax.rem(mp + outward(s, n_mp), n_mp)
        pltpu.make_async_remote_copy(
            src_ref=zsend.at[dst],
            dst_ref=zrecv.at[mp],
            send_sem=send_sem.at[0],
            recv_sem=recv_sem.at[0],
            device_id={"mp": dst},
            device_id_type=MESH,
        ).start()
        return 0

    lax.fori_loop(0, n_mp - 1, send_z, 0)
    zrecv[mp] = zsend[mp]
    wait_bytes(zrecv, n_mp - 1, recv_sem.at[0])
    mine = jnp.sum(zrecv[...], axis=0)
    fbuf[...] = mine
    xbuf[ex] = mine

    def send_x(s, _):
        dst = lax.rem(ex + outward(s, n_ex), n_ex)
        pltpu.make_async_remote_copy(
            src_ref=fbuf,
            dst_ref=xbuf.at[ex],
            send_sem=send_sem.at[1],
            recv_sem=recv_sem.at[1],
            device_id={"ex": dst},
            device_id_type=MESH,
        ).start()
        return 0

    lax.fori_loop(0, n_ex - 1, send_x, 0)

    lane = lax.broadcasted_iota(jnp.int32, (8, 2 * sketch), 1)
    turned = jnp.concatenate([mine[:, sketch:], mine[:, :sketch]], axis=1)
    lower = jnp.where(lane < sketch, mine, turned)
    upper = jnp.where(lane < sketch, turned, mine)
    for r in range(8):
        rowsend[r] = lower[r : r + 1]
        rowsend[r + 8] = upper[r : r + 1]

    def send_rows(s, _):
        dst = lax.rem(mp + outward(s, n_mp), n_mp)
        pltpu.make_async_remote_copy(
            src_ref=rowsend.at[dst],
            dst_ref=rowrecv.at[mp],
            send_sem=send_sem.at[2],
            recv_sem=recv_sem.at[2],
            device_id={"mp": dst},
            device_id_type=MESH,
        ).start()
        return 0

    lax.fori_loop(0, n_mp - 1, send_rows, 0)
    rowrecv[mp] = rowsend[mp]

    wait_bytes(xbuf, n_ex - 1, recv_sem.at[1])
    every = xbuf[...].reshape(n_ex * 8, 2 * sketch)
    square = lax.dot_general(
        every,
        every,
        (((0,), (0,)), ((), ())),
        preferred_element_type=jnp.float32,
        precision=lax.Precision.HIGHEST,
    )
    out_s[...] = (square[:sketch, :sketch] + square[sketch:, sketch:]) * (1.0 / (n_ex * 16))
    wait_bytes(rowrecv, n_mp - 1, recv_sem.at[2])
    wait_bytes(zsend, n_mp - 1, send_sem.at[0])
    wait_bytes(xbuf, n_ex - 1, send_sem.at[1])
    wait_bytes(rowsend, n_mp - 1, send_sem.at[2])


def local(n_ex, n_mp, *args):
    acts, grads, down, up, in_proj, g_proj, order, damping = args
    rank, sketch = down.shape[1], in_proj.shape[1]
    scaling = 1.0 / math.sqrt(2.0 * EXAMPLE_LENGTH * n_mp)
    f32 = jnp.float32
    vmem = pl.BlockSpec(memory_space=pltpu.VMEM)
    gram, row_parts = pl.pallas_call(
        functools.partial(kernel, n_ex, n_mp, scaling),
        out_shape=(
            jax.ShapeDtypeStruct((sketch, sketch), f32),
            jax.ShapeDtypeStruct((n_mp, 1, 2 * sketch), f32),
        ),
        in_specs=[pl.BlockSpec(memory_space=pl.ANY)] * 7,
        out_specs=(vmem, vmem),
        scratch_shapes=[
            pltpu.VMEM(acts.shape[1:], acts.dtype),
            pltpu.VMEM(grads.shape[1:], grads.dtype),
            pltpu.VMEM((rank + sketch, acts.shape[2]), acts.dtype),
            pltpu.VMEM((rank + sketch, grads.shape[2]), grads.dtype),
            pltpu.VMEM((n_mp, 8, 2 * sketch), f32),
            pltpu.VMEM((n_mp, 8, 2 * sketch), f32),
            pltpu.VMEM((8, 2 * sketch), f32),
            pltpu.VMEM((n_ex, 8, 2 * sketch), f32),
            pltpu.VMEM((n_mp, 1, 2 * sketch), f32),
            pltpu.VMEM(order.shape, order.dtype),
            pltpu.SemaphoreType.DMA((4 + 3 * CHUNKS,)),
            pltpu.SemaphoreType.DMA((3,)),
            pltpu.SemaphoreType.DMA((3,)),
        ],
        compiler_params=pltpu.CompilerParams(collective_id=0, has_side_effects=True),
        name="trak",
    )(acts, grads, down, up, in_proj, g_proj, order)
    return pl.pallas_call(
        finish,
        out_shape=(
            jax.ShapeDtypeStruct((1, rank * sketch), f32),
            jax.ShapeDtypeStruct((1, sketch, sketch), f32),
        ),
        in_specs=[vmem, vmem, pl.BlockSpec(memory_space=pltpu.SMEM)],
        out_specs=(vmem, vmem),
        name="finish",
    )(gram, row_parts, damping)


def solution(mesh):
    in_specs = (
        P("mp", "ex", None),
        P("mp", "ex", None),
        P("mp", None, None),
        P("mp", None, None),
        P("mp", None, None),
        P("mp", None, None),
        P("mp", "ex", None),
        P(),
    )
    out_specs = (P(("ex", "mp"), None), P("mp", None, None))
    body = functools.partial(local, mesh.shape["ex"], mesh.shape["mp"])
    return jax.shard_map(body, mesh=mesh, in_specs=in_specs, out_specs=out_specs, check_vma=False)
```

```python
import functools
import math

import jax
import jax.numpy as jnp
from jax import lax
from jax.experimental import pallas as pl
from jax.experimental.pallas import tpu as pltpu
from jax.sharding import PartitionSpec as P

EXAMPLE_LENGTH = 8
CHUNKS = 4
MESH = pl.DeviceIdType.MESH


def nt(a, b):
    return lax.dot_general(a, b, (((1,), (1,)), ((), ())), preferred_element_type=jnp.float32)


def halves(x):
    high = x.astype(jnp.bfloat16)
    return high, (x - high.astype(jnp.float32)).astype(jnp.bfloat16)


def outward(step, n):
    turn = lax.rem(step + 1, 2)
    return n // 2 + ((step + 1) // 2) * (1 - 2 * turn)


def wait_bytes(buf, count, sem):
    part = buf.at[pl.ds(0, count)]
    pltpu.make_async_copy(part, part, sem).wait()


def factor(blocks, r_ref, size):
    lane = lax.broadcasted_iota(jnp.int32, (8, size), 1)
    subl = lax.broadcasted_iota(jnp.int32, (8, size), 0)
    blocks = list(blocks)
    count = size // 8
    for q in range(count):
        k0 = q * 8
        top = blocks[q]
        cols = {
            b: [jnp.broadcast_to(blocks[b][:, k0 + j : k0 + j + 1], (8, size)) for j in range(8)]
            for b in range(q, count)
        }
        pivots = []
        rows = []
        scaled = []
        for j in range(8):
            pivot = jnp.broadcast_to(cols[q][j][j : j + 1, :], (8, size))
            inverse = 1.0 / pivot
            pivots.append(pivot)
            row = jnp.broadcast_to(top[j : j + 1, :], (8, size))
            step = row * inverse
            rows.append(row)
            scaled.append(step)
            top = top - cols[q][j] * step
            for i in range(j + 1, 8):
                ratio = jnp.broadcast_to(cols[q][i][j : j + 1, :], (8, size)) * inverse
                for b in range(q, count):
                    cols[b][i] = cols[b][i] - cols[b][j] * ratio
        whole, scale = rows[7], pivots[7]
        for j in range(7):
            whole = jnp.where(subl == j, rows[j], whole)
            scale = jnp.where(subl == j, pivots[j], scale)
        r_ref[0, k0 : k0 + 8, :] = jnp.where(lane >= subl + k0, whole * lax.rsqrt(scale), 0.0)
        for b in range(q + 1, count):
            for j in range(8):
                blocks[b] = blocks[b] - cols[b][j] * scaled[j]


def finish(gram, rowrecv, damping, out_f, out_r):
    size = gram.shape[0]
    diag = lax.broadcasted_iota(jnp.int32, (size, size), 0) == lax.broadcasted_iota(
        jnp.int32, (size, size), 1
    )
    full = gram[...] + jnp.where(diag, damping[0], 0.0)
    factor([full[b * 8 : b * 8 + 8] for b in range(size // 8)], out_r, size)
    low_lane = lax.broadcasted_iota(jnp.int32, (1, 2 * size), 1) < size
    for p in range(rowrecv.shape[0] // 2):
        out_f[:, p * 2 * size : (p + 1) * 2 * size] = jnp.where(
            low_lane, rowrecv[2 * p], rowrecv[2 * p + 1]
        )


def kernel(
    n_ex,
    n_mp,
    scaling,
    acts,
    grads,
    down,
    up,
    in_proj,
    g_proj,
    order,
    out_s,
    rowrecv,
    a_v,
    g_v,
    wa_v,
    wg_v,
    zsend,
    zrecv,
    fbuf,
    xbuf,
    rowsend,
    order_v,
    load_sem,
    send_sem,
    recv_sem,
):
    ex = lax.axis_index("ex")
    mp = lax.axis_index("mp")
    rank = down.shape[1]
    sketch = in_proj.shape[1]
    width = a_v.shape[1] // CHUNKS

    g_copies = [
        pltpu.make_async_copy(up.at[0], wg_v.at[pl.ds(0, rank)], load_sem.at[0]),
        pltpu.make_async_copy(g_proj.at[0], wg_v.at[pl.ds(rank, sketch)], load_sem.at[1]),
        pltpu.make_async_copy(grads.at[0], g_v, load_sem.at[2]),
    ]
    a_copies = []
    for i in range(CHUNKS):
        cols = pl.ds(i * width, width)
        a_copies.append(
            [
                pltpu.make_async_copy(
                    down.at[0, :, cols], wa_v.at[pl.ds(0, rank), cols], load_sem.at[3 + 3 * i]
                ),
                pltpu.make_async_copy(
                    in_proj.at[0, :, cols], wa_v.at[pl.ds(rank, sketch), cols], load_sem.at[4 + 3 * i]
                ),
                pltpu.make_async_copy(acts.at[0, :, cols], a_v.at[:, cols], load_sem.at[5 + 3 * i]),
            ]
        )
    order_copy = pltpu.make_async_copy(order, order_v, load_sem.at[3 + 3 * CHUNKS])

    barrier = pltpu.get_barrier_semaphore()

    def greet(axis, n, me):
        def body(s, _):
            dst = lax.rem(me + outward(s, n), n)
            pl.semaphore_signal(barrier, inc=1, device_id={axis: dst}, device_id_type=MESH)
            return 0

        lax.fori_loop(0, n - 1, body, 0)

    greet("mp", n_mp, mp)
    order_copy.start()
    for copy in g_copies:
        copy.start()
    for chunk in a_copies:
        for copy in chunk:
            copy.start()
    greet("ex", n_ex, ex)

    tokens = a_v.shape[0]
    spread = (
        lax.broadcasted_iota(jnp.int32, (rank, tokens), 1) // EXAMPLE_LENGTH
        == lax.broadcasted_iota(jnp.int32, (rank, tokens), 0)
    ).astype(jnp.float32)
    order_copy.wait()
    stored = jnp.broadcast_to(order_v[0].astype(jnp.float32), (16, 16)).astype(jnp.bfloat16)
    target = lax.dot_general(
        stored,
        spread.astype(jnp.bfloat16),
        (((1,), (0,)), ((), ())),
        preferred_element_type=jnp.float32,
    )
    rows = lax.broadcasted_iota(jnp.int32, (16, tokens), 0).astype(jnp.float32)
    place = jnp.where(target == rows, scaling, 0.0)

    for copy in g_copies:
        copy.wait()
    from_g = nt(wg_v[...], g_v[...])
    from_a = jnp.zeros((rank + sketch, tokens), jnp.float32)
    for i in range(CHUNKS):
        for copy in a_copies[i]:
            copy.wait()
        cols = slice(i * width, (i + 1) * width)
        from_a = from_a + nt(wa_v[:, cols], a_v[:, cols])

    low = [from_g[:rank], from_a[:rank]]
    left = jnp.concatenate(
        [
            jnp.concatenate(
                [
                    (x[:, None, :] * place[None, h * 8 : h * 8 + 8]).reshape(rank * 8, tokens)
                    for x in low
                ],
                axis=1,
            )
            for h in range(2)
        ],
        axis=0,
    )
    right = jnp.concatenate([from_a[rank:], from_g[rank:]], axis=1)
    left_h, left_l = halves(left)
    right_h, right_l = halves(right)
    part = nt(left_h, right_h) + (nt(left_h, right_l) + nt(left_l, right_h))
    tiles = jnp.concatenate([part[: rank * 8], part[rank * 8 :]], axis=1)
    zsend[...] = tiles.reshape(rank, 8, 2 * sketch)

    pl.semaphore_wait(barrier, n_mp + n_ex - 2)

    def send_z(s, _):
        dst = lax.rem(mp + outward(s, n_mp), n_mp)
        pltpu.make_async_remote_copy(
            src_ref=zsend.at[dst],
            dst_ref=zrecv.at[mp],
            send_sem=send_sem.at[0],
            recv_sem=recv_sem.at[0],
            device_id={"mp": dst},
            device_id_type=MESH,
        ).start()
        return 0

    lax.fori_loop(0, n_mp - 1, send_z, 0)
    zrecv[mp] = zsend[mp]
    wait_bytes(zrecv, n_mp - 1, recv_sem.at[0])
    mine = jnp.sum(zrecv[...], axis=0)
    fbuf[...] = mine
    xbuf[ex] = mine

    def send_x(s, _):
        dst = lax.rem(ex + outward(s, n_ex), n_ex)
        pltpu.make_async_remote_copy(
            src_ref=fbuf,
            dst_ref=xbuf.at[ex],
            send_sem=send_sem.at[1],
            recv_sem=recv_sem.at[1],
            device_id={"ex": dst},
            device_id_type=MESH,
        ).start()
        return 0

    lax.fori_loop(0, n_ex - 1, send_x, 0)

    lane = lax.broadcasted_iota(jnp.int32, (8, 2 * sketch), 1)
    turned = jnp.concatenate([mine[:, sketch:], mine[:, :sketch]], axis=1)
    lower = jnp.where(lane < sketch, mine, turned)
    upper = jnp.where(lane < sketch, turned, mine)
    for r in range(8):
        rowsend[r] = lower[r : r + 1]
        rowsend[r + 8] = upper[r : r + 1]

    def send_rows(s, _):
        dst = lax.rem(mp + outward(s, n_mp), n_mp)
        pltpu.make_async_remote_copy(
            src_ref=rowsend.at[dst],
            dst_ref=rowrecv.at[mp],
            send_sem=send_sem.at[2],
            recv_sem=recv_sem.at[2],
            device_id={"mp": dst},
            device_id_type=MESH,
        ).start()
        return 0

    lax.fori_loop(0, n_mp - 1, send_rows, 0)
    rowrecv[mp] = rowsend[mp]

    wait_bytes(xbuf, n_ex - 1, recv_sem.at[1])
    every = xbuf[...].reshape(n_ex * 8, 2 * sketch)
    square = lax.dot_general(
        every,
        every,
        (((0,), (0,)), ((), ())),
        preferred_element_type=jnp.float32,
        precision=lax.Precision.HIGHEST,
    )
    out_s[...] = (square[:sketch, :sketch] + square[sketch:, sketch:]) * (1.0 / (n_ex * 16))
    wait_bytes(rowrecv, n_mp - 1, recv_sem.at[2])
    wait_bytes(zsend, n_mp - 1, send_sem.at[0])
    wait_bytes(xbuf, n_ex - 1, send_sem.at[1])
    wait_bytes(rowsend, n_mp - 1, send_sem.at[2])


def local(n_ex, n_mp, *args):
    acts, grads, down, up, in_proj, g_proj, order, damping = args
    rank, sketch = down.shape[1], in_proj.shape[1]
    scaling = 1.0 / math.sqrt(2.0 * EXAMPLE_LENGTH * n_mp)
    f32 = jnp.float32
    vmem = pl.BlockSpec(memory_space=pltpu.VMEM)
    gram, row_parts = pl.pallas_call(
        functools.partial(kernel, n_ex, n_mp, scaling),
        out_shape=(
            pltpu.VMEM((sketch, sketch), f32),
            pltpu.VMEM((n_mp, 1, 2 * sketch), f32),
        ),
        in_specs=[pl.BlockSpec(memory_space=pl.ANY)] * 7,
        out_specs=(vmem, vmem),
        scratch_shapes=[
            pltpu.VMEM(acts.shape[1:], acts.dtype),
            pltpu.VMEM(grads.shape[1:], grads.dtype),
            pltpu.VMEM((rank + sketch, acts.shape[2]), acts.dtype),
            pltpu.VMEM((rank + sketch, grads.shape[2]), grads.dtype),
            pltpu.VMEM((n_mp, 8, 2 * sketch), f32),
            pltpu.VMEM((n_mp, 8, 2 * sketch), f32),
            pltpu.VMEM((8, 2 * sketch), f32),
            pltpu.VMEM((n_ex, 8, 2 * sketch), f32),
            pltpu.VMEM((n_mp, 1, 2 * sketch), f32),
            pltpu.VMEM(order.shape, order.dtype),
            pltpu.SemaphoreType.DMA((4 + 3 * CHUNKS,)),
            pltpu.SemaphoreType.DMA((3,)),
            pltpu.SemaphoreType.DMA((3,)),
        ],
        compiler_params=pltpu.CompilerParams(collective_id=0, has_side_effects=True),
        name="trak",
    )(acts, grads, down, up, in_proj, g_proj, order)
    gram = pltpu.with_memory_space_constraint(gram, pltpu.VMEM)
    row_parts = pltpu.with_memory_space_constraint(row_parts, pltpu.VMEM)
    return pl.pallas_call(
        finish,
        out_shape=(
            jax.ShapeDtypeStruct((1, rank * sketch), f32),
            jax.ShapeDtypeStruct((1, sketch, sketch), f32),
        ),
        in_specs=[vmem, vmem, pl.BlockSpec(memory_space=pltpu.SMEM)],
        out_specs=(vmem, vmem),
        name="finish",
    )(gram, row_parts, damping)


def solution(mesh):
    in_specs = (
        P("mp", "ex", None),
        P("mp", "ex", None),
        P("mp", None, None),
        P("mp", None, None),
        P("mp", None, None),
        P("mp", None, None),
        P("mp", "ex", None),
        P(),
    )
    out_specs = (P(("ex", "mp"), None), P("mp", None, None))
    body = functools.partial(local, mesh.shape["ex"], mesh.shape["mp"])
    return jax.shard_map(body, mesh=mesh, in_specs=in_specs, out_specs=out_specs, check_vma=False)
```

```python
import functools
import math

import jax
import jax.numpy as jnp
from jax import lax
from jax.experimental import pallas as pl
from jax.experimental.pallas import tpu as pltpu
from jax.sharding import PartitionSpec as P

EXAMPLE_LENGTH = 8
CHUNKS = 4
MESH = pl.DeviceIdType.MESH


def nt(a, b):
    return lax.dot_general(a, b, (((1,), (1,)), ((), ())), preferred_element_type=jnp.float32)


def halves(x):
    high = x.astype(jnp.bfloat16)
    return high, (x - high.astype(jnp.float32)).astype(jnp.bfloat16)


def outward(step, n):
    turn = lax.rem(step + 1, 2)
    return n // 2 + ((step + 1) // 2) * (1 - 2 * turn)


def wait_bytes(buf, count, sem):
    part = buf.at[pl.ds(0, count)]
    pltpu.make_async_copy(part, part, sem).wait()


def factor(blocks, r_ref, size):
    lane = lax.broadcasted_iota(jnp.int32, (8, size), 1)
    subl = lax.broadcasted_iota(jnp.int32, (8, size), 0)
    blocks = list(blocks)
    count = size // 8
    for q in range(count):
        k0 = q * 8
        top = blocks[q]
        cols = {
            b: [jnp.broadcast_to(blocks[b][:, k0 + j : k0 + j + 1], (8, size)) for j in range(8)]
            for b in range(q, count)
        }
        pivots = []
        rows = []
        scaled = []
        for j in range(8):
            pivot = jnp.broadcast_to(cols[q][j][j : j + 1, :], (8, size))
            inverse = 1.0 / pivot
            pivots.append(pivot)
            row = jnp.broadcast_to(top[j : j + 1, :], (8, size))
            step = row * inverse
            rows.append(row)
            scaled.append(step)
            top = top - cols[q][j] * step
            for i in range(j + 1, 8):
                ratio = jnp.broadcast_to(cols[q][i][j : j + 1, :], (8, size)) * inverse
                for b in range(q, count):
                    cols[b][i] = cols[b][i] - cols[b][j] * ratio
        whole, scale = rows[7], pivots[7]
        for j in range(7):
            whole = jnp.where(subl == j, rows[j], whole)
            scale = jnp.where(subl == j, pivots[j], scale)
        r_ref[0, k0 : k0 + 8, :] = jnp.where(lane >= subl + k0, whole * lax.rsqrt(scale), 0.0)
        for b in range(q + 1, count):
            for j in range(8):
                blocks[b] = blocks[b] - cols[b][j] * scaled[j]


def finish(upper, rowrecv, out_f, out_r):
    size = upper.shape[1]
    out_r[...] = upper[...]
    low_lane = lax.broadcasted_iota(jnp.int32, (1, 2 * size), 1) < size
    for p in range(rowrecv.shape[0] // 2):
        out_f[:, p * 2 * size : (p + 1) * 2 * size] = jnp.where(
            low_lane, rowrecv[2 * p], rowrecv[2 * p + 1]
        )


def kernel(
    n_ex,
    n_mp,
    scaling,
    acts,
    grads,
    down,
    up,
    in_proj,
    g_proj,
    order,
    damping,
    upper,
    rowrecv,
    a_v,
    g_v,
    wa_v,
    wg_v,
    zsend,
    zrecv,
    fbuf,
    xbuf,
    rowsend,
    order_v,
    load_sem,
    send_sem,
    recv_sem,
):
    ex = lax.axis_index("ex")
    mp = lax.axis_index("mp")
    rank = down.shape[1]
    sketch = in_proj.shape[1]
    width = a_v.shape[1] // CHUNKS

    g_copies = [
        pltpu.make_async_copy(up.at[0], wg_v.at[pl.ds(0, rank)], load_sem.at[0]),
        pltpu.make_async_copy(g_proj.at[0], wg_v.at[pl.ds(rank, sketch)], load_sem.at[1]),
        pltpu.make_async_copy(grads.at[0], g_v, load_sem.at[2]),
    ]
    a_copies = []
    for i in range(CHUNKS):
        cols = pl.ds(i * width, width)
        a_copies.append(
            [
                pltpu.make_async_copy(
                    down.at[0, :, cols], wa_v.at[pl.ds(0, rank), cols], load_sem.at[3 + 3 * i]
                ),
                pltpu.make_async_copy(
                    in_proj.at[0, :, cols], wa_v.at[pl.ds(rank, sketch), cols], load_sem.at[4 + 3 * i]
                ),
                pltpu.make_async_copy(acts.at[0, :, cols], a_v.at[:, cols], load_sem.at[5 + 3 * i]),
            ]
        )
    order_copy = pltpu.make_async_copy(order, order_v, load_sem.at[3 + 3 * CHUNKS])

    barrier = pltpu.get_barrier_semaphore()

    def greet(axis, n, me):
        def body(s, _):
            dst = lax.rem(me + outward(s, n), n)
            pl.semaphore_signal(barrier, inc=1, device_id={axis: dst}, device_id_type=MESH)
            return 0

        lax.fori_loop(0, n - 1, body, 0)

    greet("mp", n_mp, mp)
    order_copy.start()
    for copy in g_copies:
        copy.start()
    for chunk in a_copies:
        for copy in chunk:
            copy.start()
    greet("ex", n_ex, ex)

    tokens = a_v.shape[0]
    spread = (
        lax.broadcasted_iota(jnp.int32, (rank, tokens), 1) // EXAMPLE_LENGTH
        == lax.broadcasted_iota(jnp.int32, (rank, tokens), 0)
    ).astype(jnp.float32)
    order_copy.wait()
    stored = jnp.broadcast_to(order_v[0].astype(jnp.float32), (16, 16)).astype(jnp.bfloat16)
    target = lax.dot_general(
        stored,
        spread.astype(jnp.bfloat16),
        (((1,), (0,)), ((), ())),
        preferred_element_type=jnp.float32,
    )
    rows = lax.broadcasted_iota(jnp.int32, (16, tokens), 0).astype(jnp.float32)
    place = jnp.where(target == rows, scaling, 0.0)

    for copy in g_copies:
        copy.wait()
    from_g = nt(wg_v[...], g_v[...])
    from_a = jnp.zeros((rank + sketch, tokens), jnp.float32)
    for i in range(CHUNKS):
        for copy in a_copies[i]:
            copy.wait()
        cols = slice(i * width, (i + 1) * width)
        from_a = from_a + nt(wa_v[:, cols], a_v[:, cols])

    low = [from_g[:rank], from_a[:rank]]
    left = jnp.concatenate(
        [
            jnp.concatenate(
                [
                    (x[:, None, :] * place[None, h * 8 : h * 8 + 8]).reshape(rank * 8, tokens)
                    for x in low
                ],
                axis=1,
            )
            for h in range(2)
        ],
        axis=0,
    )
    right = jnp.concatenate([from_a[rank:], from_g[rank:]], axis=1)
    left_h, left_l = halves(left)
    right_h, right_l = halves(right)
    part = nt(left_h, right_h) + (nt(left_h, right_l) + nt(left_l, right_h))
    tiles = jnp.concatenate([part[: rank * 8], part[rank * 8 :]], axis=1)
    zsend[...] = tiles.reshape(rank, 8, 2 * sketch)

    pl.semaphore_wait(barrier, n_mp + n_ex - 2)

    def send_z(s, _):
        dst = lax.rem(mp + outward(s, n_mp), n_mp)
        pltpu.make_async_remote_copy(
            src_ref=zsend.at[dst],
            dst_ref=zrecv.at[mp],
            send_sem=send_sem.at[0],
            recv_sem=recv_sem.at[0],
            device_id={"mp": dst},
            device_id_type=MESH,
        ).start()
        return 0

    lax.fori_loop(0, n_mp - 1, send_z, 0)
    zrecv[mp] = zsend[mp]
    wait_bytes(zrecv, n_mp - 1, recv_sem.at[0])
    mine = jnp.sum(zrecv[...], axis=0)
    fbuf[...] = mine
    xbuf[ex] = mine

    def send_x(s, _):
        dst = lax.rem(ex + outward(s, n_ex), n_ex)
        pltpu.make_async_remote_copy(
            src_ref=fbuf,
            dst_ref=xbuf.at[ex],
            send_sem=send_sem.at[1],
            recv_sem=recv_sem.at[1],
            device_id={"ex": dst},
            device_id_type=MESH,
        ).start()
        return 0

    lax.fori_loop(0, n_ex - 1, send_x, 0)

    lane = lax.broadcasted_iota(jnp.int32, (8, 2 * sketch), 1)
    turned = jnp.concatenate([mine[:, sketch:], mine[:, :sketch]], axis=1)
    first = jnp.where(lane < sketch, mine, turned)
    second = jnp.where(lane < sketch, turned, mine)
    for r in range(8):
        rowsend[r] = first[r : r + 1]
        rowsend[r + 8] = second[r : r + 1]

    def send_rows(s, _):
        dst = lax.rem(mp + outward(s, n_mp), n_mp)
        pltpu.make_async_remote_copy(
            src_ref=rowsend.at[dst],
            dst_ref=rowrecv.at[mp],
            send_sem=send_sem.at[2],
            recv_sem=recv_sem.at[2],
            device_id={"mp": dst},
            device_id_type=MESH,
        ).start()
        return 0

    lax.fori_loop(0, n_mp - 1, send_rows, 0)
    rowrecv[mp] = rowsend[mp]

    wait_bytes(xbuf, n_ex - 1, recv_sem.at[1])
    every = xbuf[...].reshape(n_ex * 8, 2 * sketch)
    square = lax.dot_general(
        every,
        every,
        (((0,), (0,)), ((), ())),
        preferred_element_type=jnp.float32,
        precision=lax.Precision.HIGHEST,
    )
    gram = (square[:sketch, :sketch] + square[sketch:, sketch:]) * (1.0 / (n_ex * 16))
    diag = lax.broadcasted_iota(jnp.int32, (sketch, sketch), 0) == lax.broadcasted_iota(
        jnp.int32, (sketch, sketch), 1
    )
    system = gram + jnp.where(diag, damping[0], 0.0)
    factor([system[b * 8 : b * 8 + 8] for b in range(sketch // 8)], upper, sketch)
    wait_bytes(rowrecv, n_mp - 1, recv_sem.at[2])
    wait_bytes(zsend, n_mp - 1, send_sem.at[0])
    wait_bytes(xbuf, n_ex - 1, send_sem.at[1])
    wait_bytes(rowsend, n_mp - 1, send_sem.at[2])


def local(n_ex, n_mp, *args):
    acts, grads, down, up, in_proj, g_proj, order, damping = args
    rank, sketch = down.shape[1], in_proj.shape[1]
    scaling = 1.0 / math.sqrt(2.0 * EXAMPLE_LENGTH * n_mp)
    f32 = jnp.float32
    vmem = pl.BlockSpec(memory_space=pltpu.VMEM)
    triangle, row_parts = pl.pallas_call(
        functools.partial(kernel, n_ex, n_mp, scaling),
        out_shape=(
            pltpu.VMEM((1, sketch, sketch), f32),
            pltpu.VMEM((n_mp, 1, 2 * sketch), f32),
        ),
        in_specs=[pl.BlockSpec(memory_space=pl.ANY)] * 7 + [pl.BlockSpec(memory_space=pltpu.SMEM)],
        out_specs=(vmem, vmem),
        scratch_shapes=[
            pltpu.VMEM(acts.shape[1:], acts.dtype),
            pltpu.VMEM(grads.shape[1:], grads.dtype),
            pltpu.VMEM((rank + sketch, acts.shape[2]), acts.dtype),
            pltpu.VMEM((rank + sketch, grads.shape[2]), grads.dtype),
            pltpu.VMEM((n_mp, 8, 2 * sketch), f32),
            pltpu.VMEM((n_mp, 8, 2 * sketch), f32),
            pltpu.VMEM((8, 2 * sketch), f32),
            pltpu.VMEM((n_ex, 8, 2 * sketch), f32),
            pltpu.VMEM((n_mp, 1, 2 * sketch), f32),
            pltpu.VMEM(order.shape, order.dtype),
            pltpu.SemaphoreType.DMA((4 + 3 * CHUNKS,)),
            pltpu.SemaphoreType.DMA((3,)),
            pltpu.SemaphoreType.DMA((3,)),
        ],
        compiler_params=pltpu.CompilerParams(collective_id=0, has_side_effects=True),
        name="trak",
    )(acts, grads, down, up, in_proj, g_proj, order, damping)
    triangle = pltpu.with_memory_space_constraint(triangle, pltpu.VMEM)
    row_parts = pltpu.with_memory_space_constraint(row_parts, pltpu.VMEM)
    return pl.pallas_call(
        finish,
        out_shape=(
            jax.ShapeDtypeStruct((1, rank * sketch), f32),
            jax.ShapeDtypeStruct((1, sketch, sketch), f32),
        ),
        in_specs=[vmem, vmem],
        out_specs=(vmem, vmem),
        name="finish",
    )(triangle, row_parts)


def solution(mesh):
    in_specs = (
        P("mp", "ex", None),
        P("mp", "ex", None),
        P("mp", None, None),
        P("mp", None, None),
        P("mp", None, None),
        P("mp", None, None),
        P("mp", "ex", None),
        P(),
    )
    out_specs = (P(("ex", "mp"), None), P("mp", None, None))
    body = functools.partial(local, mesh.shape["ex"], mesh.shape["mp"])
    return jax.shard_map(body, mesh=mesh, in_specs=in_specs, out_specs=out_specs, check_vma=False)
```

```python
import functools
import math

import jax
import jax.numpy as jnp
from jax import lax
from jax.experimental import pallas as pl
from jax.experimental.pallas import tpu as pltpu
from jax.sharding import PartitionSpec as P

EXAMPLE_LENGTH = 8
CHUNKS = 4
MESH = pl.DeviceIdType.MESH


def nt(a, b):
    return lax.dot_general(a, b, (((1,), (1,)), ((), ())), preferred_element_type=jnp.float32)


def halves(x):
    high = x.astype(jnp.bfloat16)
    return high, (x - high.astype(jnp.float32)).astype(jnp.bfloat16)


def outward(step, n):
    turn = lax.rem(step + 1, 2)
    return n // 2 + ((step + 1) // 2) * (1 - 2 * turn)


def wait_bytes(buf, count, sem):
    part = buf.at[pl.ds(0, count)]
    pltpu.make_async_copy(part, part, sem).wait()


def factor(blocks, r_ref, size):
    lane = lax.broadcasted_iota(jnp.int32, (8, size), 1)
    subl = lax.broadcasted_iota(jnp.int32, (8, size), 0)
    blocks = list(blocks)
    count = size // 8
    for q in range(count):
        k0 = q * 8
        top = blocks[q]
        cols = {
            b: [jnp.broadcast_to(blocks[b][:, k0 + j : k0 + j + 1], (8, size)) for j in range(8)]
            for b in range(q, count)
        }
        pivots = []
        rows = []
        scaled = []
        for j in range(8):
            pivot = jnp.broadcast_to(cols[q][j][j : j + 1, :], (8, size))
            inverse = 1.0 / pivot
            pivots.append(pivot)
            row = jnp.broadcast_to(top[j : j + 1, :], (8, size))
            step = row * inverse
            rows.append(row)
            scaled.append(step)
            top = top - cols[q][j] * step
            for i in range(j + 1, 8):
                ratio = jnp.broadcast_to(cols[q][i][j : j + 1, :], (8, size)) * inverse
                for b in range(q, count):
                    cols[b][i] = cols[b][i] - cols[b][j] * ratio
        whole, scale = rows[7], pivots[7]
        for j in range(7):
            whole = jnp.where(subl == j, rows[j], whole)
            scale = jnp.where(subl == j, pivots[j], scale)
        r_ref[0, k0 : k0 + 8, :] = jnp.where(lane >= subl + k0, whole * lax.rsqrt(scale), 0.0)
        for b in range(q + 1, count):
            for j in range(8):
                blocks[b] = blocks[b] - cols[b][j] * scaled[j]


def finish(upper, rowrecv, out_f, out_r):
    size = upper.shape[1]
    out_r[...] = upper[...]
    low_lane = lax.broadcasted_iota(jnp.int32, (1, 2 * size), 1) < size
    for p in range(rowrecv.shape[0] // 2):
        out_f[:, p * 2 * size : (p + 1) * 2 * size] = jnp.where(
            low_lane, rowrecv[2 * p], rowrecv[2 * p + 1]
        )


def kernel(
    n_ex,
    n_mp,
    scaling,
    acts,
    grads,
    down,
    up,
    in_proj,
    g_proj,
    order,
    damping,
    upper,
    rowrecv,
    a_v,
    g_v,
    wa_v,
    wg_v,
    zsend,
    zrecv,
    relaysend,
    relayrecv,
    fbuf,
    xbuf,
    rowsend,
    order_v,
    load_sem,
    send_sem,
    recv_sem,
):
    ex = lax.axis_index("ex")
    mp = lax.axis_index("mp")
    rank = down.shape[1]
    sketch = in_proj.shape[1]
    width = a_v.shape[1] // CHUNKS

    g_copies = [
        pltpu.make_async_copy(up.at[0], wg_v.at[pl.ds(0, rank)], load_sem.at[0]),
        pltpu.make_async_copy(g_proj.at[0], wg_v.at[pl.ds(rank, sketch)], load_sem.at[1]),
        pltpu.make_async_copy(grads.at[0], g_v, load_sem.at[2]),
    ]
    a_copies = []
    for i in range(CHUNKS):
        cols = pl.ds(i * width, width)
        a_copies.append(
            [
                pltpu.make_async_copy(
                    down.at[0, :, cols], wa_v.at[pl.ds(0, rank), cols], load_sem.at[3 + 3 * i]
                ),
                pltpu.make_async_copy(
                    in_proj.at[0, :, cols], wa_v.at[pl.ds(rank, sketch), cols], load_sem.at[4 + 3 * i]
                ),
                pltpu.make_async_copy(acts.at[0, :, cols], a_v.at[:, cols], load_sem.at[5 + 3 * i]),
            ]
        )
    order_copy = pltpu.make_async_copy(order, order_v, load_sem.at[3 + 3 * CHUNKS])

    barrier = pltpu.get_barrier_semaphore()

    def greet(axis, n, me):
        def body(s, _):
            dst = lax.rem(me + outward(s, n), n)
            pl.semaphore_signal(barrier, inc=1, device_id={axis: dst}, device_id_type=MESH)
            return 0

        lax.fori_loop(0, n - 1, body, 0)

    for far in range(n_mp // 4, 0, -1):
        for dst in (lax.rem(mp + far, n_mp), lax.rem(mp + n_mp - far, n_mp)):
            pl.semaphore_signal(barrier, inc=1, device_id={"mp": dst}, device_id_type=MESH)
    order_copy.start()
    for copy in g_copies:
        copy.start()
    for chunk in a_copies:
        for copy in chunk:
            copy.start()
    greet("ex", n_ex, ex)

    tokens = a_v.shape[0]
    spread = (
        lax.broadcasted_iota(jnp.int32, (rank, tokens), 1) // EXAMPLE_LENGTH
        == lax.broadcasted_iota(jnp.int32, (rank, tokens), 0)
    ).astype(jnp.float32)
    order_copy.wait()
    stored = jnp.broadcast_to(order_v[0].astype(jnp.float32), (16, 16)).astype(jnp.bfloat16)
    target = lax.dot_general(
        stored,
        spread.astype(jnp.bfloat16),
        (((1,), (0,)), ((), ())),
        preferred_element_type=jnp.float32,
    )
    rows = lax.broadcasted_iota(jnp.int32, (16, tokens), 0).astype(jnp.float32)
    place = jnp.where(target == rows, scaling, 0.0)

    for copy in g_copies:
        copy.wait()
    from_g = nt(wg_v[...], g_v[...])
    from_a = jnp.zeros((rank + sketch, tokens), jnp.float32)
    for i in range(CHUNKS):
        for copy in a_copies[i]:
            copy.wait()
        cols = slice(i * width, (i + 1) * width)
        from_a = from_a + nt(wa_v[:, cols], a_v[:, cols])

    low = [from_g[:rank], from_a[:rank]]
    left = jnp.concatenate(
        [
            jnp.concatenate(
                [
                    (x[:, None, :] * place[None, h * 8 : h * 8 + 8]).reshape(rank * 8, tokens)
                    for x in low
                ],
                axis=1,
            )
            for h in range(2)
        ],
        axis=0,
    )
    right = jnp.concatenate([from_a[rank:], from_g[rank:]], axis=1)
    left_h, left_l = halves(left)
    right_h, right_l = halves(right)
    part = nt(left_h, right_h) + (nt(left_h, right_l) + nt(left_l, right_h))
    tiles = jnp.concatenate([part[: rank * 8], part[rank * 8 :]], axis=1)
    half = n_mp // 2
    for c in range(rank):
        zsend[c % half, c // half] = tiles[c * 8 : c * 8 + 8]

    reach = half // 2
    pl.semaphore_wait(barrier, 2 * reach + n_ex - 1)

    offsets = [a for far in range(reach, 0, -1) for a in (far, -far) if a != -reach]
    for k, a in enumerate(offsets):
        relay = lax.rem(mp + n_mp - a, n_mp)
        pltpu.make_async_remote_copy(
            src_ref=zsend.at[lax.rem(relay + reach, half)],
            dst_ref=zrecv.at[k],
            send_sem=send_sem.at[0],
            recv_sem=recv_sem.at[0],
            device_id={"mp": relay},
            device_id_type=MESH,
        ).start()
    group = lax.rem(mp + reach, half)
    total = zsend[group]
    wait_bytes(zrecv, len(offsets), recv_sem.at[0])
    relaysend[...] = total + jnp.sum(zrecv[...], axis=0)
    for q in range(2):
        pltpu.make_async_remote_copy(
            src_ref=relaysend.at[q],
            dst_ref=relayrecv.at[mp // half],
            send_sem=send_sem.at[3],
            recv_sem=recv_sem.at[3],
            device_id={"mp": group + q * half},
            device_id_type=MESH,
        ).start()
    wait_bytes(relayrecv, 2, recv_sem.at[3])
    mine = relayrecv[0] + relayrecv[1]
    fbuf[...] = mine
    xbuf[ex] = mine

    def send_x(s, _):
        dst = lax.rem(ex + outward(s, n_ex), n_ex)
        pltpu.make_async_remote_copy(
            src_ref=fbuf,
            dst_ref=xbuf.at[ex],
            send_sem=send_sem.at[1],
            recv_sem=recv_sem.at[1],
            device_id={"ex": dst},
            device_id_type=MESH,
        ).start()
        return 0

    lax.fori_loop(0, n_ex - 1, send_x, 0)

    lane = lax.broadcasted_iota(jnp.int32, (8, 2 * sketch), 1)
    turned = jnp.concatenate([mine[:, sketch:], mine[:, :sketch]], axis=1)
    first = jnp.where(lane < sketch, mine, turned)
    second = jnp.where(lane < sketch, turned, mine)
    for r in range(8):
        rowsend[r] = first[r : r + 1]
        rowsend[r + 8] = second[r : r + 1]

    def send_rows(s, _):
        dst = lax.rem(mp + outward(s, n_mp), n_mp)
        pltpu.make_async_remote_copy(
            src_ref=rowsend.at[dst],
            dst_ref=rowrecv.at[mp],
            send_sem=send_sem.at[2],
            recv_sem=recv_sem.at[2],
            device_id={"mp": dst},
            device_id_type=MESH,
        ).start()
        return 0

    lax.fori_loop(0, n_mp - 1, send_rows, 0)
    rowrecv[mp] = rowsend[mp]

    wait_bytes(xbuf, n_ex - 1, recv_sem.at[1])
    every = xbuf[...].reshape(n_ex * 8, 2 * sketch)
    square = lax.dot_general(
        every,
        every,
        (((0,), (0,)), ((), ())),
        preferred_element_type=jnp.float32,
        precision=lax.Precision.HIGHEST,
    )
    gram = (square[:sketch, :sketch] + square[sketch:, sketch:]) * (1.0 / (n_ex * 16))
    diag = lax.broadcasted_iota(jnp.int32, (sketch, sketch), 0) == lax.broadcasted_iota(
        jnp.int32, (sketch, sketch), 1
    )
    system = gram + jnp.where(diag, damping[0], 0.0)
    factor([system[b * 8 : b * 8 + 8] for b in range(sketch // 8)], upper, sketch)
    wait_bytes(rowrecv, n_mp - 1, recv_sem.at[2])
    wait_bytes(zrecv, n_mp // 2 - 1, send_sem.at[0])
    wait_bytes(relaysend, 2, send_sem.at[3])
    wait_bytes(xbuf, n_ex - 1, send_sem.at[1])
    wait_bytes(rowsend, n_mp - 1, send_sem.at[2])


def local(n_ex, n_mp, *args):
    acts, grads, down, up, in_proj, g_proj, order, damping = args
    rank, sketch = down.shape[1], in_proj.shape[1]
    scaling = 1.0 / math.sqrt(2.0 * EXAMPLE_LENGTH * n_mp)
    f32 = jnp.float32
    vmem = pl.BlockSpec(memory_space=pltpu.VMEM)
    triangle, row_parts = pl.pallas_call(
        functools.partial(kernel, n_ex, n_mp, scaling),
        out_shape=(
            pltpu.VMEM((1, sketch, sketch), f32),
            pltpu.VMEM((n_mp, 1, 2 * sketch), f32),
        ),
        in_specs=[pl.BlockSpec(memory_space=pl.ANY)] * 7 + [pl.BlockSpec(memory_space=pltpu.SMEM)],
        out_specs=(vmem, vmem),
        scratch_shapes=[
            pltpu.VMEM(acts.shape[1:], acts.dtype),
            pltpu.VMEM(grads.shape[1:], grads.dtype),
            pltpu.VMEM((rank + sketch, acts.shape[2]), acts.dtype),
            pltpu.VMEM((rank + sketch, grads.shape[2]), grads.dtype),
            pltpu.VMEM((n_mp // 2, 2, 8, 2 * sketch), f32),
            pltpu.VMEM((n_mp // 2 - 1, 2, 8, 2 * sketch), f32),
            pltpu.VMEM((2, 8, 2 * sketch), f32),
            pltpu.VMEM((2, 8, 2 * sketch), f32),
            pltpu.VMEM((8, 2 * sketch), f32),
            pltpu.VMEM((n_ex, 8, 2 * sketch), f32),
            pltpu.VMEM((n_mp, 1, 2 * sketch), f32),
            pltpu.VMEM(order.shape, order.dtype),
            pltpu.SemaphoreType.DMA((4 + 3 * CHUNKS,)),
            pltpu.SemaphoreType.DMA((4,)),
            pltpu.SemaphoreType.DMA((4,)),
        ],
        compiler_params=pltpu.CompilerParams(collective_id=0, has_side_effects=True),
        name="trak",
    )(acts, grads, down, up, in_proj, g_proj, order, damping)
    triangle = pltpu.with_memory_space_constraint(triangle, pltpu.VMEM)
    row_parts = pltpu.with_memory_space_constraint(row_parts, pltpu.VMEM)
    return pl.pallas_call(
        finish,
        out_shape=(
            jax.ShapeDtypeStruct((1, rank * sketch), f32),
            jax.ShapeDtypeStruct((1, sketch, sketch), f32),
        ),
        in_specs=[vmem, vmem],
        out_specs=(vmem, vmem),
        name="finish",
    )(triangle, row_parts)


def solution(mesh):
    in_specs = (
        P("mp", "ex", None),
        P("mp", "ex", None),
        P("mp", None, None),
        P("mp", None, None),
        P("mp", None, None),
        P("mp", None, None),
        P("mp", "ex", None),
        P(),
    )
    out_specs = (P(("ex", "mp"), None), P("mp", None, None))
    body = functools.partial(local, mesh.shape["ex"], mesh.shape["mp"])
    return jax.shard_map(body, mesh=mesh, in_specs=in_specs, out_specs=out_specs, check_vma=False)
```

```python
import functools
import math

import jax
import jax.numpy as jnp
from jax import lax
from jax.experimental import pallas as pl
from jax.experimental.pallas import tpu as pltpu
from jax.sharding import PartitionSpec as P

EXAMPLE_LENGTH = 8
CHUNKS = 4
MESH = pl.DeviceIdType.MESH


def nt(a, b):
    return lax.dot_general(a, b, (((1,), (1,)), ((), ())), preferred_element_type=jnp.float32)


def halves(x):
    high = x.astype(jnp.bfloat16)
    return high, (x - high.astype(jnp.float32)).astype(jnp.bfloat16)


def outward(step, n):
    turn = (step + 1) % 2
    return n // 2 + ((step + 1) // 2) * (1 - 2 * turn)


def wait_bytes(buf, count, sem):
    part = buf.at[pl.ds(0, count)]
    pltpu.make_async_copy(part, part, sem).wait()


def factor(blocks, r_ref, size):
    lane = lax.broadcasted_iota(jnp.int32, (8, size), 1)
    subl = lax.broadcasted_iota(jnp.int32, (8, size), 0)
    blocks = list(blocks)
    count = size // 8
    for q in range(count):
        k0 = q * 8
        top = blocks[q]
        cols = {
            b: [jnp.broadcast_to(blocks[b][:, k0 + j : k0 + j + 1], (8, size)) for j in range(8)]
            for b in range(q, count)
        }
        pivots = []
        rows = []
        scaled = []
        for j in range(8):
            pivot = jnp.broadcast_to(cols[q][j][j : j + 1, :], (8, size))
            inverse = 1.0 / pivot
            pivots.append(pivot)
            row = jnp.broadcast_to(top[j : j + 1, :], (8, size))
            step = row * inverse
            rows.append(row)
            scaled.append(step)
            top = top - cols[q][j] * step
            for i in range(j + 1, 8):
                ratio = jnp.broadcast_to(cols[q][i][j : j + 1, :], (8, size)) * inverse
                for b in range(q, count):
                    cols[b][i] = cols[b][i] - cols[b][j] * ratio
        whole, scale = rows[7], pivots[7]
        for j in range(7):
            whole = jnp.where(subl == j, rows[j], whole)
            scale = jnp.where(subl == j, pivots[j], scale)
        r_ref[0, k0 : k0 + 8, :] = jnp.where(lane >= subl + k0, whole * lax.rsqrt(scale), 0.0)
        for b in range(q + 1, count):
            for j in range(8):
                blocks[b] = blocks[b] - cols[b][j] * scaled[j]


def finish(upper, rowrecv, out_f, out_r):
    size = upper.shape[1]
    out_r[...] = upper[...]
    low_lane = lax.broadcasted_iota(jnp.int32, (1, 2 * size), 1) < size
    for p in range(rowrecv.shape[0] // 2):
        out_f[:, p * 2 * size : (p + 1) * 2 * size] = jnp.where(
            low_lane, rowrecv[2 * p], rowrecv[2 * p + 1]
        )


def kernel(
    n_ex,
    n_mp,
    scaling,
    acts,
    grads,
    down,
    up,
    in_proj,
    g_proj,
    order,
    damping,
    upper,
    rowrecv,
    a_v,
    g_v,
    wa_v,
    wg_v,
    zsend,
    zrecv,
    relaysend,
    relayrecv,
    fbuf,
    xbuf,
    rowsend,
    order_v,
    load_sem,
    send_sem,
    recv_sem,
):
    ex = lax.axis_index("ex")
    mp = lax.axis_index("mp")
    rank = down.shape[1]
    sketch = in_proj.shape[1]
    width = a_v.shape[1] // CHUNKS

    g_copies = [
        pltpu.make_async_copy(up.at[0], wg_v.at[pl.ds(0, rank)], load_sem.at[0]),
        pltpu.make_async_copy(g_proj.at[0], wg_v.at[pl.ds(rank, sketch)], load_sem.at[1]),
        pltpu.make_async_copy(grads.at[0], g_v, load_sem.at[2]),
    ]
    a_copies = []
    for i in range(CHUNKS):
        cols = pl.ds(i * width, width)
        a_copies.append(
            [
                pltpu.make_async_copy(
                    down.at[0, :, cols], wa_v.at[pl.ds(0, rank), cols], load_sem.at[3 + 3 * i]
                ),
                pltpu.make_async_copy(
                    in_proj.at[0, :, cols], wa_v.at[pl.ds(rank, sketch), cols], load_sem.at[4 + 3 * i]
                ),
                pltpu.make_async_copy(acts.at[0, :, cols], a_v.at[:, cols], load_sem.at[5 + 3 * i]),
            ]
        )
    order_copy = pltpu.make_async_copy(order, order_v, load_sem.at[3 + 3 * CHUNKS])

    barrier = pltpu.get_barrier_semaphore()

    def greet(axis, n, me):
        def body(s, _):
            dst = lax.rem(me + outward(s, n), n)
            pl.semaphore_signal(barrier, inc=1, device_id={axis: dst}, device_id_type=MESH)
            return 0

        lax.fori_loop(0, n - 1, body, 0)

    for far in range(n_mp // 4, 0, -1):
        for dst in (lax.rem(mp + far, n_mp), lax.rem(mp + n_mp - far, n_mp)):
            pl.semaphore_signal(barrier, inc=1, device_id={"mp": dst}, device_id_type=MESH)
    order_copy.start()
    for copy in g_copies:
        copy.start()
    for chunk in a_copies:
        for copy in chunk:
            copy.start()
    greet("ex", n_ex, ex)

    tokens = a_v.shape[0]
    spread = (
        lax.broadcasted_iota(jnp.int32, (rank, tokens), 1) // EXAMPLE_LENGTH
        == lax.broadcasted_iota(jnp.int32, (rank, tokens), 0)
    ).astype(jnp.float32)
    order_copy.wait()
    stored = jnp.broadcast_to(order_v[0].astype(jnp.float32), (16, 16)).astype(jnp.bfloat16)
    target = lax.dot_general(
        stored,
        spread.astype(jnp.bfloat16),
        (((1,), (0,)), ((), ())),
        preferred_element_type=jnp.float32,
    )
    rows = lax.broadcasted_iota(jnp.int32, (16, tokens), 0).astype(jnp.float32)
    place = jnp.where(target == rows, scaling, 0.0)

    for copy in g_copies:
        copy.wait()
    from_g = nt(wg_v[...], g_v[...])
    from_a = jnp.zeros((rank + sketch, tokens), jnp.float32)
    for i in range(CHUNKS):
        for copy in a_copies[i]:
            copy.wait()
        cols = slice(i * width, (i + 1) * width)
        from_a = from_a + nt(wa_v[:, cols], a_v[:, cols])

    low = [from_g[:rank], from_a[:rank]]
    left = jnp.concatenate(
        [
            jnp.concatenate(
                [
                    (x[:, None, :] * place[None, h * 8 : h * 8 + 8]).reshape(rank * 8, tokens)
                    for x in low
                ],
                axis=1,
            )
            for h in range(2)
        ],
        axis=0,
    )
    right = jnp.concatenate([from_a[rank:], from_g[rank:]], axis=1)
    left_h, left_l = halves(left)
    right_h, right_l = halves(right)
    part = nt(left_h, right_h) + (nt(left_h, right_l) + nt(left_l, right_h))
    tiles = jnp.concatenate([part[: rank * 8], part[rank * 8 :]], axis=1)
    half = n_mp // 2
    for c in range(rank):
        zsend[c % half, c // half] = tiles[c * 8 : c * 8 + 8]

    reach = half // 2
    pl.semaphore_wait(barrier, 2 * reach + n_ex - 1)

    offsets = [a for far in range(reach, 0, -1) for a in (far, -far) if a != -reach]
    for k, a in enumerate(offsets):
        relay = lax.rem(mp + n_mp - a, n_mp)
        pltpu.make_async_remote_copy(
            src_ref=zsend.at[lax.rem(relay + reach, half)],
            dst_ref=zrecv.at[k],
            send_sem=send_sem.at[0],
            recv_sem=recv_sem.at[0],
            device_id={"mp": relay},
            device_id_type=MESH,
        ).start()
    group = lax.rem(mp + reach, half)
    total = zsend[group]
    wait_bytes(zrecv, len(offsets), recv_sem.at[0])
    relaysend[...] = total + jnp.sum(zrecv[...], axis=0)
    for q in range(2):
        pltpu.make_async_remote_copy(
            src_ref=relaysend.at[q],
            dst_ref=relayrecv.at[mp // half],
            send_sem=send_sem.at[3],
            recv_sem=recv_sem.at[3],
            device_id={"mp": group + q * half},
            device_id_type=MESH,
        ).start()
    wait_bytes(relayrecv, 2, recv_sem.at[3])
    mine = relayrecv[0] + relayrecv[1]
    fbuf[...] = mine
    xbuf[ex] = mine

    def send_x(s, _):
        dst = lax.rem(ex + outward(s, n_ex), n_ex)
        pltpu.make_async_remote_copy(
            src_ref=fbuf,
            dst_ref=xbuf.at[ex],
            send_sem=send_sem.at[1],
            recv_sem=recv_sem.at[1],
            device_id={"ex": dst},
            device_id_type=MESH,
        ).start()
        return 0

    for s in range(n_ex - 1):
        send_x(s, 0)

    lane = lax.broadcasted_iota(jnp.int32, (8, 2 * sketch), 1)
    turned = jnp.concatenate([mine[:, sketch:], mine[:, :sketch]], axis=1)
    first = jnp.where(lane < sketch, mine, turned)
    second = jnp.where(lane < sketch, turned, mine)
    for r in range(8):
        rowsend[r] = first[r : r + 1]
        rowsend[r + 8] = second[r : r + 1]

    def send_rows(s, _):
        dst = lax.rem(mp + outward(s, n_mp), n_mp)
        pltpu.make_async_remote_copy(
            src_ref=rowsend.at[dst],
            dst_ref=rowrecv.at[mp],
            send_sem=send_sem.at[2],
            recv_sem=recv_sem.at[2],
            device_id={"mp": dst},
            device_id_type=MESH,
        ).start()
        return 0

    lax.fori_loop(0, n_mp - 1, send_rows, 0)
    rowrecv[mp] = rowsend[mp]

    wait_bytes(xbuf, n_ex - 1, recv_sem.at[1])
    every = xbuf[...].reshape(n_ex * 8, 2 * sketch)
    square = lax.dot_general(
        every,
        every,
        (((0,), (0,)), ((), ())),
        preferred_element_type=jnp.float32,
        precision=lax.Precision.HIGHEST,
    )
    gram = (square[:sketch, :sketch] + square[sketch:, sketch:]) * (1.0 / (n_ex * 16))
    diag = lax.broadcasted_iota(jnp.int32, (sketch, sketch), 0) == lax.broadcasted_iota(
        jnp.int32, (sketch, sketch), 1
    )
    system = gram + jnp.where(diag, damping[0], 0.0)
    factor([system[b * 8 : b * 8 + 8] for b in range(sketch // 8)], upper, sketch)
    wait_bytes(rowrecv, n_mp - 1, recv_sem.at[2])
    wait_bytes(zrecv, n_mp // 2 - 1, send_sem.at[0])
    wait_bytes(relaysend, 2, send_sem.at[3])
    wait_bytes(xbuf, n_ex - 1, send_sem.at[1])
    wait_bytes(rowsend, n_mp - 1, send_sem.at[2])


def local(n_ex, n_mp, *args):
    acts, grads, down, up, in_proj, g_proj, order, damping = args
    rank, sketch = down.shape[1], in_proj.shape[1]
    scaling = 1.0 / math.sqrt(2.0 * EXAMPLE_LENGTH * n_mp)
    f32 = jnp.float32
    vmem = pl.BlockSpec(memory_space=pltpu.VMEM)
    triangle, row_parts = pl.pallas_call(
        functools.partial(kernel, n_ex, n_mp, scaling),
        out_shape=(
            pltpu.VMEM((1, sketch, sketch), f32),
            pltpu.VMEM((n_mp, 1, 2 * sketch), f32),
        ),
        in_specs=[pl.BlockSpec(memory_space=pl.ANY)] * 7 + [pl.BlockSpec(memory_space=pltpu.SMEM)],
        out_specs=(vmem, vmem),
        scratch_shapes=[
            pltpu.VMEM(acts.shape[1:], acts.dtype),
            pltpu.VMEM(grads.shape[1:], grads.dtype),
            pltpu.VMEM((rank + sketch, acts.shape[2]), acts.dtype),
            pltpu.VMEM((rank + sketch, grads.shape[2]), grads.dtype),
            pltpu.VMEM((n_mp // 2, 2, 8, 2 * sketch), f32),
            pltpu.VMEM((n_mp // 2 - 1, 2, 8, 2 * sketch), f32),
            pltpu.VMEM((2, 8, 2 * sketch), f32),
            pltpu.VMEM((2, 8, 2 * sketch), f32),
            pltpu.VMEM((8, 2 * sketch), f32),
            pltpu.VMEM((n_ex, 8, 2 * sketch), f32),
            pltpu.VMEM((n_mp, 1, 2 * sketch), f32),
            pltpu.VMEM(order.shape, order.dtype),
            pltpu.SemaphoreType.DMA((4 + 3 * CHUNKS,)),
            pltpu.SemaphoreType.DMA((4,)),
            pltpu.SemaphoreType.DMA((4,)),
        ],
        compiler_params=pltpu.CompilerParams(collective_id=0, has_side_effects=True),
        name="trak",
    )(acts, grads, down, up, in_proj, g_proj, order, damping)
    triangle = pltpu.with_memory_space_constraint(triangle, pltpu.VMEM)
    row_parts = pltpu.with_memory_space_constraint(row_parts, pltpu.VMEM)
    return pl.pallas_call(
        finish,
        out_shape=(
            jax.ShapeDtypeStruct((1, rank * sketch), f32),
            jax.ShapeDtypeStruct((1, sketch, sketch), f32),
        ),
        in_specs=[vmem, vmem],
        out_specs=(vmem, vmem),
        name="finish",
    )(triangle, row_parts)


def solution(mesh):
    in_specs = (
        P("mp", "ex", None),
        P("mp", "ex", None),
        P("mp", None, None),
        P("mp", None, None),
        P("mp", None, None),
        P("mp", None, None),
        P("mp", "ex", None),
        P(),
    )
    out_specs = (P(("ex", "mp"), None), P("mp", None, None))
    body = functools.partial(local, mesh.shape["ex"], mesh.shape["mp"])
    return jax.shard_map(body, mesh=mesh, in_specs=in_specs, out_specs=out_specs, check_vma=False)
```
